32 devices in a mesh: row: 8 (over y, x, core), col: 4 (over z).
Axes of the slice: x: 2, y: 2, z: 4, core: 2. Of those that a mesh axis runs over, the one named last changes fastest.
Arguments:
- student_in: bfloat16 [768, 8192], P('col', 'row'), may hold values from -6 to 6
- norm_gain: bfloat16 [8192], P('row'), may hold values from 0.099609375 to 1.8984375
- w_gate: bfloat16 [8192, 28672], P('row', 'col'), may hold values from -0.0625 to 0.0625
- w_up: bfloat16 [8192, 28672], P('row', 'col'), may hold values from -0.0625 to 0.0625
- w_down: bfloat16 [28672, 8192], P('col', 'row'), may hold values from -0.03125 to 0.03125
- teacher: bfloat16 [2, 768, 8192], P(None, 'col', 'row'), may hold values from -6 to 6
- layer_map: int32 [2], replicated, may hold values from 0 to 1, each once
Outputs:
- student_out: bfloat16 [768, 8192], P('col', 'row')
- match_loss: float32 [], replicated
The draws below stay inside these ranges and needn't reach their ends.
Inputs may be any that keep to these rules, and one draw needn't show every extreme that they name: `layer_map`: a permutation of 0 to 1.
All inputs are finite; a program needn't handle non-finite values.
Results may differ from the reference program's by a relative error of at most 0.014.
Values may be sent and summed in bfloat16 or wider, within the bound.
A program may use at most 192 MiB of HBM per device.

```python
import jax
import jax.numpy as jnp
from jax import lax

D = 8192
FF = 28672
TEACH = 2
TOKENS = 768
N_ROW = 8
N_COL = 4


def level_of(key, shape, split, smallest, top_value):
    factor_of = 1.0
    for position, parts in split:
        heights = jax.random.uniform(jax.random.fold_in(jax.random.fold_in(key, 6), position), (parts,), jnp.float32, smallest / len(split), top_value / len(split))
        factor_of = factor_of * jnp.repeat(jnp.exp(heights), shape[position] // parts).reshape((-1,) + (1,) * (len(shape) - 1 - position))
    return factor_of


def gaussian(rng, extent, deviation, most, pieces=(), dtype=jnp.bfloat16):
    loudness = level_of(rng, extent, pieces, -0.22, 0.18) if pieces else 1.0
    array = jax.random.normal(rng, extent, jnp.float32) * deviation * loudness
    return jnp.minimum(jnp.maximum(array, -most), most).astype(dtype)


def setup_inputs(seed: int = 0) -> dict:
    streams_of = jax.random.split(jax.random.key(seed), 8)
    return {
        "student_in": gaussian(streams_of[0], (TOKENS, D), 1.0, 6.0, ((0, 4), (1, 8))),
        "norm_gain": jnp.clip(1.0 + 0.18 * jax.random.normal(streams_of[1], (D,), jnp.float32), 0.099609375, 1.8984375).astype(jnp.bfloat16),
        "w_gate": gaussian(streams_of[2], (D, FF), D ** -0.5, 0.0625, ((0, 8), (1, 4))),
        "w_up": gaussian(streams_of[3], (D, FF), D ** -0.5, 0.0625, ((0, 8), (1, 4))),
        "w_down": gaussian(streams_of[4], (FF, D), FF ** -0.5, 0.03125, ((0, 4), (1, 8))),
        "teacher": gaussian(streams_of[5], (TEACH, TOKENS, D), 1.0, 6.0, ((1, 4), (2, 8))),
        "layer_map": jax.random.permutation(streams_of[6], TEACH).astype(jnp.int32),
    }


def reference(student_in, norm_gain, w_gate, w_up, w_down, teacher, layer_map):
    xf = student_in.astype(jnp.float32)
    mean_sq = lax.optimization_barrier(jnp.mean(xf * xf, axis=1, keepdims=True))
    normed = (xf * jax.lax.rsqrt(mean_sq + 1e-05) * norm_gain.astype(jnp.float32)[None, :]).astype(jnp.bfloat16)
    feat_block = D // N_ROW
    gate = jnp.zeros((normed.shape[0], FF), jnp.float32)
    up = jnp.zeros((normed.shape[0], FF), jnp.float32)
    for index in range(N_ROW):
        cols = normed[:, index * feat_block:(index + 1) * feat_block]
        gate = gate + jnp.dot(cols, w_gate[index * feat_block:(index + 1) * feat_block], preferred_element_type=jnp.float32).astype(jnp.bfloat16).astype(jnp.float32)
        up = up + jnp.dot(cols, w_up[index * feat_block:(index + 1) * feat_block], preferred_element_type=jnp.float32).astype(jnp.bfloat16).astype(jnp.float32)
    hidden = (jax.nn.silu(gate) * up).astype(jnp.bfloat16)
    hid_block = FF // N_COL
    branch = jnp.zeros((normed.shape[0], D), jnp.float32)
    for index in range(N_COL):
        part = jnp.dot(hidden[:, index * hid_block:(index + 1) * hid_block], w_down[index * hid_block:(index + 1) * hid_block], preferred_element_type=jnp.float32)
        branch = branch + part.astype(jnp.bfloat16).astype(jnp.float32)
    student_out = (xf + branch).astype(jnp.bfloat16)
    target = jax.lax.dynamic_index_in_dim(teacher, layer_map[0].astype(jnp.int32), 0, keepdims=False).astype(jnp.float32)
    diff = student_out.astype(jnp.float32) - target
    match_loss = jnp.mean(diff * diff)
    return (student_out, match_loss)
```

```python
import functools

import jax
import jax.numpy as jnp
from jax import lax
from jax.experimental import pallas as pl
from jax.experimental.pallas import tpu as pltpu
from jax.sharding import PartitionSpec as P

BF = jnp.bfloat16
F32 = jnp.float32


def kernel(nr, nz, w, total, x_ref, gain_ref, wg_ref, wu_ref, wd_ref, teacher_ref, map_ref,
           out_ref, loss_ref,
           x_all, xg, ss, ssr, scale, wgu, wdn, p_own, p_send, s_in, half_send, half_in,
           full_send, full_in, h_all, acc, cs_r, cs_l, cr_r, cr_l, lsum, l_row, l_col,
           x_sems, w_sem, wd_sem, ss_sems, sib_sems, rs_send, rs_recv, ag_send, ag_recv,
           hs_send, hs_recv, c_sems, l_sems):
    n = nr // 2
    hn = n // 2
    chunks = s_in.shape[0]
    tr, feat = x_ref.shape
    g = tr * nz // nr
    hg = g // 2
    r = lax.axis_index("row")
    z = lax.axis_index("col")
    core = lax.rem(r, 2)
    chip = lax.div(r, 2)
    a, b = lax.div(chip, 2), lax.rem(chip, 2)
    pos = a + b * (n - 1 - 2 * a)

    def chip_at(off):
        q = lax.rem(pos + (off % n), n)
        far = lax.div(q, hn)
        return far * (2 * (n - 1 - q) + 1) + (1 - far) * 2 * q

    me = chip_at(0)
    sibling = {"row": chip * 2 + 1 - core}
    ring = ({"row": chip_at(1) * 2 + core}, {"row": chip_at(-1) * 2 + core})
    sign = (1, -1)
    rows_of = (pl.ds(0, hg), pl.ds(hg, hg))

    def remote(src, dst, send, recv, dev):
        return pltpu.make_async_remote_copy(
            src_ref=src, dst_ref=dst, send_sem=send, recv_sem=recv,
            device_id=dev, device_id_type=pl.DeviceIdType.MESH)

    barrier = pltpu.get_barrier_semaphore()
    for d in range(1, nr):
        pl.semaphore_signal(barrier, inc=1, device_id={"row": lax.rem(r + d, nr)},
                            device_id_type=pl.DeviceIdType.MESH)
    for d in range(1, nz):
        pl.semaphore_signal(barrier, inc=1, device_id={"col": lax.rem(z + d, nz)},
                            device_id_type=pl.DeviceIdType.MESH)
    pl.semaphore_wait(barrier, nr - 1 + nz - 1)

    def up_load(j):
        slot = lax.rem(j, 2)
        cols = pl.ds(pl.multiple_of(j * w, w), w)
        return (pltpu.make_async_copy(wg_ref.at[:, cols], wgu.at[slot, :, pl.ds(0, w)], w_sem.at[slot, 0]),
                pltpu.make_async_copy(wu_ref.at[:, cols], wgu.at[slot, :, pl.ds(w, w)], w_sem.at[slot, 1]))

    def down_load(j):
        slot = lax.rem(j, 2)
        return pltpu.make_async_copy(wd_ref.at[pl.ds(pl.multiple_of(j * w, w), w)], wdn.at[slot], wd_sem.at[slot])

    for c in up_load(jnp.int32(0)):
        c.start()
    down_load(jnp.int32(0)).start()

    gain = gain_ref[...].astype(F32)

    def absorb(src, blk):
        xf = src[...].astype(F32)
        rows = pl.ds(pl.multiple_of(blk * tr, tr), tr)
        xg[rows, :] = (xf * gain).astype(BF)
        sq = xf * xf
        part = sq[:, 0:128]
        for c in range(1, feat // 128):
            part = part + sq[:, c * 128:(c + 1) * 128]
        ss[rows, :] = part

    def x_copy(s, d):
        blk = z - s * sign[d]
        src = x_ref if s == 0 else x_all.at[blk]
        return remote(src, x_all.at[blk], x_sems.at[0, d, s], x_sems.at[1, d, s], {"col": z + sign[d]})

    def x_sends(s, d):
        return (z < nz - 1) & (z - s >= 0) if d == 0 else (z > 0) & (z + s <= nz - 1)

    def x_gets(s, d):
        return z - 1 - s >= 0 if d == 0 else z + 1 + s <= nz - 1

    def x_wait(s, d):
        blk = z - (s + 1) * sign[d]
        remote(x_all.at[blk], x_all.at[blk], x_sems.at[0, d, s], x_sems.at[1, d, s],
               {"col": z - sign[d]}).wait_recv()

    for s in range(nz - 1):
        for d in range(2):
            @pl.when(x_sends(s, d))
            def _():
                x_copy(s, d).start()
        if s == 0:
            absorb(x_ref, z)
        else:
            for d in range(2):
                @pl.when(x_gets(s - 1, d))
                def _():
                    absorb(x_all.at[z - s * sign[d]], z - s * sign[d])
        for d in range(2):
            @pl.when(x_gets(s, d))
            def _():
                x_wait(s, d)
    for d in range(2):
        @pl.when(x_gets(nz - 2, d))
        def _():
            absorb(x_all.at[z - (nz - 1) * sign[d]], z - (nz - 1) * sign[d])

    def ss_copy(d):
        peer = lax.rem(r + d, nr)
        return remote(ss.at[pl.ds(pl.multiple_of(peer * g, g), g)], ssr.at[d - 1],
                      ss_sems.at[0, d - 1], ss_sems.at[1, d - 1], {"row": peer})

    for d in range(1, nr):
        ss_copy(d).start()

    def sib(j):
        slot = lax.rem(j, 2)
        return remote(p_send.at[slot], s_in.at[j], sib_sems.at[slot], sib_sems.at[2 + j], sibling)

    def rs(s, d, j):
        slot = lax.rem(j, 2)
        if s == 0:
            src, dst = half_send.at[slot, d], half_in.at[j, d]
        else:
            src, dst = full_send.at[slot, s - 1, d], full_in.at[j, s - 1, d]
        return remote(src, dst, rs_send.at[s, d, slot], rs_recv.at[s, d, j], ring[d])

    def ag(s, d, j, got=False):
        blk = chip_at(-sign[d] * (s + 1 if got else s))
        ref = h_all.at[j, blk, core]
        if s == hn - 1:
            ref = h_all.at[j, blk, core, rows_of[d]]
        return remote(ref, ref, ag_send.at[s, d, lax.rem(j, 2)], ag_recv.at[s, d, j], ring[d])

    def hs(off, j, got=False):
        ref = h_all.at[j, chip_at(off), 1 - core if got else core]
        return remote(ref, ref, hs_send.at[off % n, lax.rem(j, 2)], hs_recv.at[off % n, j], sibling)

    def free(make, j):
        @pl.when(j >= 2)
        def _():
            make(j - 2).wait_send()

    def mine(j, off, rows=slice(None)):
        q = chip_at(off)
        return (p_own[lax.rem(j, hn + 2), q, rows, :].astype(F32) + s_in[j, q, rows, :].astype(F32))

    def first(j):
        slot = lax.rem(j, 2)

        @pl.when(j + 1 < chunks)
        def _():
            for c in up_load(j + 1):
                c.start()
        for c in up_load(j):
            c.wait()
        free(sib, j)
        tile = 256

        @pl.loop(0, 2 * w // tile)
        def _(t):
            cols = pl.ds(pl.multiple_of(t * tile, tile), tile)
            res = jnp.dot(xg[...], wgu[slot, :, cols], preferred_element_type=F32).astype(BF)
            res = res.reshape(n, 2, g, tile)

            @pl.when(core == 0)
            def _():
                p_own[lax.rem(j, hn + 2), :, :, cols] = res[:, 0]
                p_send[slot, :, :, cols] = res[:, 1]

            @pl.when(core == 1)
            def _():
                p_own[lax.rem(j, hn + 2), :, :, cols] = res[:, 1]
                p_send[slot, :, :, cols] = res[:, 0]
        sib(j).start()

    def reduce_step(s, j):
        slot = lax.rem(j, 2)
        if s == 0:
            sib(j).wait_recv()
        for d in range(2):
            free(functools.partial(rs, s, d), j)
            off = sign[d] * (hn - s)
            if s == 0:
                half_send[slot, d] = mine(j, off, rows_of[d]).astype(BF)
            else:
                rs(s - 1, d, j).wait_recv()
                if s == 1:
                    full_send[slot, 0, d, rows_of[1 - d]] = mine(j, off, rows_of[1 - d]).astype(BF)
                    full_send[slot, 0, d, rows_of[d]] = (
                        mine(j, off, rows_of[d]) + half_in[j, d].astype(F32)).astype(BF)
                else:
                    full_send[slot, s - 1, d] = (mine(j, off) + full_in[j, s - 2, d].astype(F32)).astype(BF)
            rs(s, d, j).start()

    def activate(j):
        @pl.when(j == 0)
        def _():
            sq = ss[pl.ds(pl.multiple_of(r * g, g), g), :]
            for d in range(1, nr):
                ss_copy(d).wait_recv()
                sq = sq + ssr[d - 1]
            mean = jnp.sum(sq, axis=1, keepdims=True) / total
            scale[...] = jnp.broadcast_to(lax.rsqrt(mean + 1e-5), scale.shape)
        for d in range(2):
            rs(hn - 1, d, j).wait_recv()
        val = mine(j, 0) + full_in[j, hn - 2, 0].astype(F32) + full_in[j, hn - 2, 1].astype(F32)
        val = val * scale[:, 0:1]
        gate, up = val[:, :w], val[:, w:]
        h_all[j, me, core] = (gate / (1.0 + jnp.exp(-gate)) * up).astype(BF)
        for d in range(2):
            free(functools.partial(ag, 0, d), j)
            ag(0, d, j).start()
        free(functools.partial(hs, 0), j)
        hs(0, j).start()

    def gather_step(s, j):
        for d in range(2):
            ag(s - 1, d, j, True).wait_recv()
            free(functools.partial(ag, s, d), j)
            ag(s, d, j).start()
            free(functools.partial(hs, -sign[d] * s), j)
            hs(-sign[d] * s, j).start()

    def gather_last(j):
        for d in range(2):
            ag(hn - 1, d, j, True).wait_recv()
        free(functools.partial(hs, hn), j)
        hs(hn, j).start()

    def down(j):
        slot = lax.rem(j, 2)

        @pl.when(j + 1 < chunks)
        def _():
            down_load(j + 1).start()
        down_load(j).wait()
        for off in range(n):
            hs(off, j, True).wait_recv()
        tile = 256

        @pl.loop(0, feat // tile)
        def _(t):
            cols = pl.ds(pl.multiple_of(t * tile, tile), tile)
            lhs = h_all[j].reshape(nr * g, w)
            res = jnp.dot(lhs, wdn[slot, :, cols], preferred_element_type=F32)
            acc[:, cols] += res

    acc[...] = jnp.zeros_like(acc)
    stages = [functools.partial(reduce_step, s) for s in range(hn)] + [activate]
    stages += [functools.partial(gather_step, s) for s in range(1, hn)] + [gather_last]
    order = [(1 + i, f) for i, f in enumerate(stages)]
    order += [(0, first), (1 + len(stages), down)]
    last = 1 + len(stages)

    @pl.loop(0, chunks + last)
    def _(t):
        for lag, stage in order:
            @pl.when((t >= lag) & (t - lag < chunks))
            def _():
                stage(t - lag)

    for j in (chunks - 2, chunks - 1):
        j = jnp.int32(j)
        sib(j).wait_send()
        for d in range(2):
            for s in range(hn):
                rs(s, d, j).wait_send()
                ag(s, d, j).wait_send()
        for off in range(n):
            hs(off, j).wait_send()

    def block(d):
        return pl.ds(pl.multiple_of(d * tr, tr), tr)

    def c_copy(s, d):
        src, dst = (cs_r, cr_r) if d == 0 else (cs_l, cr_l)
        return remote(src.at[s], dst.at[s], c_sems.at[0, d, s], c_sems.at[1, d, s], {"col": z + sign[d]})

    def c_wait(s, d):
        dst = cr_r if d == 0 else cr_l
        remote(dst.at[s], dst.at[s], c_sems.at[0, d, s], c_sems.at[1, d, s], {"col": z - sign[d]}).wait_recv()

    for s in range(nz - 1):
        for d in range(2):
            dest = nz - 1 - s if d == 0 else s
            src, got = (cs_r, cr_r) if d == 0 else (cs_l, cr_l)
            sends = z < dest if d == 0 else z > dest
            edge = z == (0 if d == 0 else nz - 1)

            @pl.when(sends & edge)
            def _():
                src[s] = acc[dest * tr:(dest + 1) * tr, :].astype(BF)
                c_copy(s, d).start()

            @pl.when(sends & jnp.logical_not(edge))
            def _():
                c_wait(s, d)
                src[s] = (acc[dest * tr:(dest + 1) * tr, :] + got[s].astype(F32)).astype(BF)
                c_copy(s, d).start()

    @pl.when(z > 0)
    def _():
        c_wait(nz - 1 - z, 0)
        acc[block(z), :] += cr_r[nz - 1 - z].astype(F32)

    @pl.when(z < nz - 1)
    def _():
        c_wait(z, 1)
        acc[block(z), :] += cr_l[z].astype(F32)

    out = (x_ref[...].astype(F32) + acc[block(z), :]).astype(BF)
    out_ref[...] = out
    diff = out.astype(F32) - teacher_ref[map_ref[0]].astype(F32)
    sq = jnp.sum((diff * diff).reshape(tr // 8, 8, feat), axis=0)
    part = sq[:, 0:128]
    for c in range(1, feat // 128):
        part = part + sq[:, c * 128:(c + 1) * 128]

    def l_copy(axis, d):
        size, at = (nr, r) if axis == "row" else (nz, z)
        src, dst = (lsum.at[0], l_row) if axis == "row" else (lsum.at[1], l_col)
        base = 0 if axis == "row" else nr - 1
        return remote(src, dst.at[d - 1], l_sems.at[0, base + d - 1], l_sems.at[1, base + d - 1],
                      {axis: lax.rem(at + d, size)})

    lsum[0] = part
    for d in range(1, nr):
        l_copy("row", d).start()
    for d in range(1, nr):
        l_copy("row", d).wait_recv()
        part = part + l_row[d - 1]
    lsum[1] = part
    for d in range(1, nz):
        l_copy("col", d).start()
    for d in range(1, nz):
        l_copy("col", d).wait_recv()
        part = part + l_col[d - 1]
    loss_ref[...] = part

    for d in range(1, nr):
        l_copy("row", d).wait_send()
        ss_copy(d).wait_send()
    for d in range(1, nz):
        l_copy("col", d).wait_send()
    for s in range(nz - 1):
        for d in range(2):
            @pl.when(x_sends(s, d))
            def _():
                x_copy(s, d).wait_send()
            dest = nz - 1 - s if d == 0 else s

            @pl.when(z < dest if d == 0 else z > dest)
            def _():
                c_copy(s, d).wait_send()


def body(nr, nz, student_in, norm_gain, w_gate, w_up, w_down, teacher, layer_map):
    tr, feat = student_in.shape
    ff = w_gate.shape[1]
    n, hn = nr // 2, nr // 4
    g = tr * nz // nr
    w = next(v for v in (512, 256, 128) if ff % v == 0)
    c = ff // w
    vm, dma = pltpu.VMEM, pltpu.SemaphoreType.DMA
    spec = pl.BlockSpec(memory_space=pltpu.VMEM)
    hbm = pl.BlockSpec(memory_space=pl.ANY)
    out, loss = pl.pallas_call(
        functools.partial(kernel, nr, nz, w, feat * nr),
        out_shape=(jax.ShapeDtypeStruct((tr, feat), BF), jax.ShapeDtypeStruct((8, 128), F32)),
        in_specs=[spec, spec, hbm, hbm, hbm, spec, pl.BlockSpec(memory_space=pltpu.SMEM)],
        out_specs=(spec, spec),
        scratch_shapes=[
            vm((nz, tr, feat), BF),
            vm((nz * tr, feat), BF),
            vm((nz * tr, 128), F32),
            vm((nr - 1, g, 128), F32),
            vm((g, 128), F32),
            vm((2, feat, 2 * w), BF),
            vm((2, w, feat), BF),
            vm((hn + 2, n, g, 2 * w), BF),
            vm((2, n, g, 2 * w), BF),
            vm((c, n, g, 2 * w), BF),
            vm((2, 2, g // 2, 2 * w), BF),
            vm((c, 2, g // 2, 2 * w), BF),
            vm((2, hn - 1, 2, g, 2 * w), BF),
            vm((c, hn - 1, 2, g, 2 * w), BF),
            vm((c, n, 2, g, w), BF),
            vm((nz * tr, feat), F32),
            vm((nz - 1, tr, feat), BF),
            vm((nz - 1, tr, feat), BF),
            vm((nz - 1, tr, feat), BF),
            vm((nz - 1, tr, feat), BF),
            vm((2, 8, 128), F32),
            vm((nr - 1, 8, 128), F32),
            vm((nz - 1, 8, 128), F32),
            dma((2, 2, nz - 1)),
            dma((2, 2)),
            dma((2,)),
            dma((2, nr - 1)),
            dma((2 + c,)),
            dma((hn, 2, 2)),
            dma((hn, 2, c)),
            dma((hn, 2, 2)),
            dma((hn, 2, c)),
            dma((n, 2)),
            dma((n, c)),
            dma((2, 2, nz - 1)),
            dma((2, nr + nz - 2)),
        ],
        compiler_params=pltpu.CompilerParams(
            collective_id=0, has_side_effects=True, vmem_limit_bytes=67043328),
    )(student_in, norm_gain.reshape(1, feat), w_gate, w_up, w_down, teacher, layer_map)
    return out, jnp.sum(loss) / (tr * nz * feat * nr)


def solution(mesh):
    placed = (
        P("col", "row"),
        P("row"),
        P("row", "col"),
        P("row", "col"),
        P("col", "row"),
        P(None, "col", "row"),
        P(),
    )
    return jax.shard_map(
        functools.partial(body, mesh.shape["row"], mesh.shape["col"]),
        mesh=mesh, in_specs=placed, out_specs=(P("col", "row"), P()), check_vma=False
    )
```

```python
import functools

import jax
import jax.numpy as jnp
from jax import lax
from jax.experimental import pallas as pl
from jax.experimental.pallas import tpu as pltpu
from jax.sharding import PartitionSpec as P

BF = jnp.bfloat16
F32 = jnp.float32


def kernel(nr, nz, w, total, x_ref, gain_ref, wg_ref, wu_ref, wd_ref, teacher_ref, map_ref,
           out_ref, loss_ref,
           x_all, xg, ss, ssr, scale, wgu, wdn, p_own, p_send, s_in, half_send, half_in,
           full_send, full_in, h_all, acc, cs_r, cs_l, cr_r, cr_l, lsum, l_row, l_col,
           x_sems, w_sem, wd_sem, ss_sems, sib_sems, rs_send, rs_recv, ag_send, ag_recv,
           hs_send, hs_recv, c_sems, l_sems):
    chunks = s_in.shape[0]
    n = nr // 2
    hn = n // 2
    tr, feat = x_ref.shape
    th = tr // 2
    cn = chunks // 2
    g = th * nz // nr
    step = max(1, cn // (nz - 1))
    r = lax.axis_index("row")
    z = lax.axis_index("col")
    core = lax.rem(r, 2)
    chip = lax.div(r, 2)
    a, b = lax.div(chip, 2), lax.rem(chip, 2)
    pos = a + b * (n - 1 - 2 * a)

    def chip_at(off):
        q = lax.rem(pos + (off % n), n)
        far = lax.div(q, hn)
        return far * (2 * (n - 1 - q) + 1) + (1 - far) * 2 * q

    me = chip_at(0)
    sibling = {"row": chip * 2 + 1 - core}
    ring = ({"row": chip_at(1) * 2 + core}, {"row": chip_at(-1) * 2 + core})
    sign = (1, -1)
    pair_of = (slice(0, w), slice(w, 2 * w))
    unit_of = (pl.ds(0, w // 2), pl.ds(w // 2, w // 2))

    def remote(src, dst, send, recv, dev):
        return pltpu.make_async_remote_copy(
            src_ref=src, dst_ref=dst, send_sem=send, recv_sem=recv,
            device_id=dev, device_id_type=pl.DeviceIdType.MESH)

    barrier = pltpu.get_barrier_semaphore()
    for d in range(1, nr):
        pl.semaphore_signal(barrier, inc=1, device_id={"row": lax.rem(r + d, nr)},
                            device_id_type=pl.DeviceIdType.MESH)
    for d in range(1, nz):
        pl.semaphore_signal(barrier, inc=1, device_id={"col": lax.rem(z + d, nz)},
                            device_id_type=pl.DeviceIdType.MESH)
    pl.semaphore_wait(barrier, nr - 1 + nz - 1)

    def up_load(j):
        slot = lax.rem(j, 2)
        cols = pl.ds(pl.multiple_of(lax.rem(j, cn) * w, w), w)
        return (pltpu.make_async_copy(wg_ref.at[:, cols], wgu.at[slot, :, pl.ds(0, w)], w_sem.at[slot, 0]),
                pltpu.make_async_copy(wu_ref.at[:, cols], wgu.at[slot, :, pl.ds(w, w)], w_sem.at[slot, 1]))

    def down_load(j):
        slot = lax.rem(j, 2)
        return pltpu.make_async_copy(wd_ref.at[pl.ds(pl.multiple_of(lax.rem(j, cn) * w, w), w)], wdn.at[slot], wd_sem.at[slot])

    for c in up_load(jnp.int32(0)):
        c.start()
    down_load(jnp.int32(0)).start()

    gain = gain_ref[...].astype(F32)

    def own(hf):
        return x_ref.at[pl.ds(hf * th, th)]

    def absorb(src, hf, blk):
        xf = src[...].astype(F32)
        rows = pl.ds(pl.multiple_of(blk * th, th), th)
        xg[hf, rows, :] = (xf * gain).astype(BF)
        sq = xf * xf
        part = sq[:, 0:128]
        for c in range(1, feat // 128):
            part = part + sq[:, c * 128:(c + 1) * 128]
        ss[hf, rows, :] = part

    def x_copy(hf, s, d):
        blk = z - s * sign[d]
        src = own(hf) if s == 0 else x_all.at[hf, blk]
        return remote(src, x_all.at[hf, blk], x_sems.at[0, hf, d, s], x_sems.at[1, hf, d, s],
                      {"col": z + sign[d]})

    def x_sends(s, d):
        return (z < nz - 1) & (z - s >= 0) if d == 0 else (z > 0) & (z + s <= nz - 1)

    def x_gets(s, d):
        return z - 1 - s >= 0 if d == 0 else z + 1 + s <= nz - 1

    def x_wait(hf, s, d):
        ref = x_all.at[hf, z - (s + 1) * sign[d]]
        remote(ref, ref, x_sems.at[0, hf, d, s], x_sems.at[1, hf, d, s], {"col": z - sign[d]}).wait_recv()

    def x_step(hf, s):
        for d in range(2):
            if s > 0:
                @pl.when(x_gets(s - 1, d))
                def _():
                    x_wait(hf, s - 1, d)
            if s < nz - 1:
                @pl.when(x_sends(s, d))
                def _():
                    x_copy(hf, s, d).start()

    def x_absorb(hf, s):
        if s == 0:
            absorb(own(hf), hf, z)
        else:
            for d in range(2):
                @pl.when(x_gets(s - 1, d))
                def _():
                    absorb(x_all.at[hf, z - s * sign[d]], hf, z - s * sign[d])

    def ss_copy(hf, d):
        peer = lax.rem(r + d, nr)
        return remote(ss.at[hf, pl.ds(pl.multiple_of(peer * g, g), g)], ssr.at[hf, d - 1],
                      ss_sems.at[0, hf, d - 1], ss_sems.at[1, hf, d - 1], {"row": peer})

    def ss_start(hf):
        for d in range(1, nr):
            ss_copy(hf, d).start()

    for s in range(nz):
        x_step(0, s)
        if s == nz - 1:
            x_step(1, 0)
        x_absorb(0, s)
        if s == 0:
            x_absorb(1, 0)
            acc[...] = jnp.zeros_like(acc)
    ss_start(0)

    def sib(j):
        slot = lax.rem(j, 2)
        return remote(p_send.at[slot], s_in.at[j], sib_sems.at[slot], sib_sems.at[2 + j], sibling)

    def rs(s, d, j):
        slot = lax.rem(j, 2)
        if s == 0:
            src, dst = half_send.at[slot, d], half_in.at[j, d]
        else:
            src, dst = full_send.at[slot, s - 1, d], full_in.at[j, s - 1, d]
        return remote(src, dst, rs_send.at[s, d, slot], rs_recv.at[s, d, j], ring[d])

    def ag(s, d, j, got=False):
        blk = chip_at(-sign[d] * (s + 1 if got else s))
        ref = h_all.at[j, blk, core]
        if s == hn - 1:
            ref = h_all.at[j, blk, core, :, unit_of[d]]
        return remote(ref, ref, ag_send.at[s, d, lax.rem(j, 2)], ag_recv.at[s, d, j], ring[d])

    def hs(off, j, got=False):
        ref = h_all.at[j, chip_at(off), 1 - core if got else core]
        return remote(ref, ref, hs_send.at[off % n, lax.rem(j, 2)], hs_recv.at[off % n, j], sibling)

    def free(make, j):
        @pl.when(j >= 2)
        def _():
            make(j - 2).wait_send()

    def mine(j, off, cols=slice(None)):
        q = chip_at(off)
        return (p_own[lax.rem(j, hn + 2), q, :, cols].astype(F32) + s_in[j, q, :, cols].astype(F32))

    def first(j):
        slot = lax.rem(j, 2)

        @pl.when(j + 1 < chunks)
        def _():
            for c in up_load(j + 1):
                c.start()
        for c in up_load(j):
            c.wait()
        free(sib, j)
        tile = 256

        @pl.loop(0, 2 * w // tile)
        def _(t):
            cols = pl.ds(pl.multiple_of(t * tile, tile), tile)
            res = jnp.dot(xg[lax.div(j, cn)], wgu[slot, :, cols], preferred_element_type=F32).astype(BF)
            res = res.reshape(n, 2, g, tile)

            @pl.when(core == 0)
            def _():
                p_own[lax.rem(j, hn + 2), :, :, cols] = res[:, 0]
                p_send[slot, :, :, cols] = res[:, 1]

            @pl.when(core == 1)
            def _():
                p_own[lax.rem(j, hn + 2), :, :, cols] = res[:, 1]
                p_send[slot, :, :, cols] = res[:, 0]
        sib(j).start()

    def reduce_step(s, j):
        slot = lax.rem(j, 2)
        if s == 0:
            sib(j).wait_recv()
        for d in range(2):
            free(functools.partial(rs, s, d), j)
            off = sign[d] * (hn - s)
            if s == 0:
                half_send[slot, d] = mine(j, off, pair_of[d]).astype(BF)
            else:
                rs(s - 1, d, j).wait_recv()
                if s == 1:
                    full_send[slot, 0, d, :, pair_of[1 - d]] = mine(j, off, pair_of[1 - d]).astype(BF)
                    full_send[slot, 0, d, :, pair_of[d]] = (
                        mine(j, off, pair_of[d]) + half_in[j, d].astype(F32)).astype(BF)
                else:
                    full_send[slot, s - 1, d] = (mine(j, off) + full_in[j, s - 2, d].astype(F32)).astype(BF)
            rs(s, d, j).start()

    def activate(j):
        for hf in range(2):
            @pl.when(j == hf * cn)
            def _():
                sq = ss[hf, pl.ds(pl.multiple_of(r * g, g), g), :]
                for d in range(1, nr):
                    ss_copy(hf, d).wait_recv()
                    sq = sq + ssr[hf, d - 1]
                mean = jnp.sum(sq, axis=1, keepdims=True) / total
                scale[hf] = jnp.broadcast_to(lax.rsqrt(mean + 1e-5), (g, 128))
        for d in range(2):
            rs(hn - 1, d, j).wait_recv()
        val = mine(j, 0) + full_in[j, hn - 2, 0].astype(F32) + full_in[j, hn - 2, 1].astype(F32)
        val = val * scale[lax.div(j, cn)][:, 0:1]
        gate, up = val[:, :w], val[:, w:]
        h_all[j, me, core] = (gate / (1.0 + jnp.exp(-gate)) * up).astype(BF)
        for d in range(2):
            free(functools.partial(ag, 0, d), j)
            ag(0, d, j).start()
        free(functools.partial(hs, 0), j)
        hs(0, j).start()

    def gather_step(s, j):
        for d in range(2):
            ag(s - 1, d, j, True).wait_recv()
            free(functools.partial(ag, s, d), j)
            ag(s, d, j).start()
            free(functools.partial(hs, -sign[d] * s), j)
            hs(-sign[d] * s, j).start()

    def gather_last(j):
        for d in range(2):
            ag(hn - 1, d, j, True).wait_recv()
        free(functools.partial(hs, hn), j)
        hs(hn, j).start()

    def down(j):
        slot = lax.rem(j, 2)

        @pl.when(j + 1 < chunks)
        def _():
            down_load(j + 1).start()
        down_load(j).wait()
        for off in range(n):
            hs(off, j, True).wait_recv()
        tile = 256

        @pl.loop(0, feat // tile)
        def _(t):
            cols = pl.ds(pl.multiple_of(t * tile, tile), tile)
            lhs = h_all[j].reshape(nr * g, w)
            res = jnp.dot(lhs, wdn[slot, :, cols], preferred_element_type=F32)
            acc[lax.div(j, cn), :, cols] += res

    stages = [functools.partial(reduce_step, s) for s in range(hn)] + [activate]
    stages += [functools.partial(gather_step, s) for s in range(1, hn)] + [gather_last]
    order = [(1 + i, f) for i, f in enumerate(stages)]
    order += [(0, first), (1 + len(stages), down)]
    last = 1 + len(stages)

    def c_refs(hf, d):
        return (cs_r.at[hf], cr_r.at[hf]) if d == 0 else (cs_l.at[hf], cr_l.at[hf])

    def c_copy(hf, s, d):
        src, dst = c_refs(hf, d)
        return remote(src.at[s], dst.at[s], c_sems.at[0, hf, d, s], c_sems.at[1, hf, d, s], {"col": z + sign[d]})

    def c_wait(hf, s, d):
        dst = c_refs(hf, d)[1]
        remote(dst.at[s], dst.at[s], c_sems.at[0, hf, d, s], c_sems.at[1, hf, d, s],
               {"col": z - sign[d]}).wait_recv()

    def c_sends(s, d):
        return z < nz - 1 - s if d == 0 else z > s

    def c_step(hf, s, d):
        dest = nz - 1 - s if d == 0 else s
        src, got = c_refs(hf, d)
        edge = z == (0 if d == 0 else nz - 1)

        @pl.when(c_sends(s, d) & edge)
        def _():
            src[s] = acc[hf, dest * th:(dest + 1) * th, :].astype(BF)
            c_copy(hf, s, d).start()

        @pl.when(c_sends(s, d) & jnp.logical_not(edge))
        def _():
            c_wait(hf, s, d)
            src[s] = (acc[hf, dest * th:(dest + 1) * th, :] + got[s].astype(F32)).astype(BF)
            c_copy(hf, s, d).start()

    def c_last(hf):
        block = pl.ds(pl.multiple_of(z * th, th), th)

        @pl.when(z > 0)
        def _():
            c_wait(hf, nz - 1 - z, 0)
            acc[hf, block, :] += cr_r[hf, nz - 1 - z].astype(F32)

        @pl.when(z < nz - 1)
        def _():
            c_wait(hf, z, 1)
            acc[hf, block, :] += cr_l[hf, z].astype(F32)

        rows = slice(hf * th, (hf + 1) * th)
        out = (x_ref[rows, :].astype(F32) + acc[hf, block, :]).astype(BF)
        out_ref[rows, :] = out
        diff = out.astype(F32) - teacher_ref[map_ref[0], rows, :].astype(F32)
        sq = jnp.sum((diff * diff).reshape(th // 8, 8, feat), axis=0)
        part = sq[:, 0:128]
        for c in range(1, feat // 128):
            part = part + sq[:, c * 128:(c + 1) * 128]
        return part

    pace = cn // (2 * nz - 3)

    @pl.loop(0, chunks + last)
    def _(t):
        for s in range(1, nz):
            @pl.when(t == s * step)
            def _():
                x_step(1, s)
                x_absorb(1, s)
                if s == nz - 1:
                    ss_start(1)
        for lag, stage in order:
            @pl.when((t >= lag) & (t - lag < chunks))
            def _():
                stage(t - lag)
        for s in range(nz - 1):
            for d in range(2):
                hop = z if d == 0 else nz - 1 - z
                at = pace * (s + hop) if pace > 0 else s

                @pl.when(t == cn + last + at)
                def _():
                    c_step(0, s, d)

    for s in range(nz - 1):
        for d in range(2):
            c_step(1, s, d)
        if s == 0:
            part = c_last(0)
    part = part + c_last(1)

    def l_copy(axis, d):
        size, at = (nr, r) if axis == "row" else (nz, z)
        src, dst = (lsum.at[0], l_row) if axis == "row" else (lsum.at[1], l_col)
        base = 0 if axis == "row" else nr - 1
        return remote(src, dst.at[d - 1], l_sems.at[0, base + d - 1], l_sems.at[1, base + d - 1],
                      {axis: lax.rem(at + d, size)})

    lsum[0] = part
    for d in range(1, nr):
        l_copy("row", d).start()
    for d in range(1, nr):
        l_copy("row", d).wait_recv()
        part = part + l_row[d - 1]
    lsum[1] = part
    for d in range(1, nz):
        l_copy("col", d).start()
    for d in range(1, nz):
        l_copy("col", d).wait_recv()
        part = part + l_col[d - 1]
    loss_ref[...] = part

    for d in range(1, nr):
        l_copy("row", d).wait_send()
        for hf in range(2):
            ss_copy(hf, d).wait_send()
    for d in range(1, nz):
        l_copy("col", d).wait_send()
    for s in range(nz - 1):
        for d in range(2):
            @pl.when(x_sends(s, d))
            def _():
                for hf in range(2):
                    x_copy(hf, s, d).wait_send()

            @pl.when(c_sends(s, d))
            def _():
                for hf in range(2):
                    c_copy(hf, s, d).wait_send()
    for j in (chunks - 2, chunks - 1):
        j = jnp.int32(j)
        sib(j).wait_send()
        for d in range(2):
            for s in range(hn):
                rs(s, d, j).wait_send()
                ag(s, d, j).wait_send()
        for off in range(n):
            hs(off, j).wait_send()


def body(nr, nz, student_in, norm_gain, w_gate, w_up, w_down, teacher, layer_map):
    tr, feat = student_in.shape
    ff = w_gate.shape[1]
    n, hn = nr // 2, nr // 4
    th = tr // 2
    g = th * nz // nr
    w = next(v for v in (512, 256, 128) if ff % v == 0)
    c = 2 * (ff // w)
    vm, dma = pltpu.VMEM, pltpu.SemaphoreType.DMA
    spec = pl.BlockSpec(memory_space=pltpu.VMEM)
    hbm = pl.BlockSpec(memory_space=pl.ANY)
    out, loss = pl.pallas_call(
        functools.partial(kernel, nr, nz, w, feat * nr),
        out_shape=(jax.ShapeDtypeStruct((tr, feat), BF), jax.ShapeDtypeStruct((8, 128), F32)),
        in_specs=[spec, spec, hbm, hbm, hbm, spec, pl.BlockSpec(memory_space=pltpu.SMEM)],
        out_specs=(spec, spec),
        scratch_shapes=[
            vm((2, nz, th, feat), BF),
            vm((2, nz * th, feat), BF),
            vm((2, nz * th, 128), F32),
            vm((2, nr - 1, g, 128), F32),
            vm((2, g, 128), F32),
            vm((2, feat, 2 * w), BF),
            vm((2, w, feat), BF),
            vm((hn + 2, n, g, 2 * w), BF),
            vm((2, n, g, 2 * w), BF),
            vm((c, n, g, 2 * w), BF),
            vm((2, 2, g, w), BF),
            vm((c, 2, g, w), BF),
            vm((2, hn - 1, 2, g, 2 * w), BF),
            vm((c, hn - 1, 2, g, 2 * w), BF),
            vm((c, n, 2, g, w), BF),
            vm((2, nz * th, feat), F32),
            vm((2, nz - 1, th, feat), BF),
            vm((2, nz - 1, th, feat), BF),
            vm((2, nz - 1, th, feat), BF),
            vm((2, nz - 1, th, feat), BF),
            vm((2, 8, 128), F32),
            vm((nr - 1, 8, 128), F32),
            vm((nz - 1, 8, 128), F32),
            dma((2, 2, 2, nz - 1)),
            dma((2, 2)),
            dma((2,)),
            dma((2, 2, nr - 1)),
            dma((2 + c,)),
            dma((hn, 2, 2)),
            dma((hn, 2, c)),
            dma((hn, 2, 2)),
            dma((hn, 2, c)),
            dma((n, 2)),
            dma((n, c)),
            dma((2, 2, 2, nz - 1)),
            dma((2, nr + nz - 2)),
        ],
        compiler_params=pltpu.CompilerParams(
            collective_id=0, has_side_effects=True, vmem_limit_bytes=67043328),
    )(student_in, norm_gain.reshape(1, feat), w_gate, w_up, w_down, teacher, layer_map)
    return out, jnp.sum(loss) / (tr * nz * feat * nr)


def solution(mesh):
    placed = (
        P("col", "row"),
        P("row"),
        P("row", "col"),
        P("row", "col"),
        P("col", "row"),
        P(None, "col", "row"),
        P(),
    )
    return jax.shard_map(
        functools.partial(body, mesh.shape["row"], mesh.shape["col"]),
        mesh=mesh, in_specs=placed, out_specs=(P("col", "row"), P()), check_vma=False
    )
```
